32 devices in a mesh: gx: 2 (over x), gy: 4 (over z), gz: 4 (over y, core).
Axes of the slice: x: 2, y: 2, z: 4, core: 2. Of those that a mesh axis runs over, the one named last changes fastest.
Arguments:
- volume: float32 [16, 8, 64, 512], P(None, 'gx', 'gy', 'gz'), may hold values from -26 to 26
- weight: float32 [16, 16, 3, 3, 3], replicated, may hold values from -0.3125 to 0.3125
- gamma: float32 [16], replicated, may hold values from 0.5 to 1.5
- beta: float32 [16], replicated, may hold values from -0.5 to 0.5
- cotangent: float32 [16, 8, 64, 512], P(None, 'gx', 'gy', 'gz'), may hold values from -6 to 6
Outputs:
- input_grad: float32 [16, 8, 64, 512], P(None, 'gx', 'gy', 'gz')
- weight_grad: float32 [16, 16, 3, 3, 3], replicated
- gamma_grad: float32 [16], replicated
- beta_grad: float32 [16], replicated
The draws below stay inside these ranges and needn't reach their ends.
All inputs are finite; a program needn't handle non-finite values.
Results may differ from the reference program's by a relative error of at most 0.0003.
Values sent between devices are 32-bit elements; how exact they have to be, the bound alone decides.
No kernel may reach another device: no remote copies, remote signals or barrier semaphores. Data moves between devices by JAX's collectives and lax.ppermute only.
A program may use at most 64 MiB of HBM per device.

```python
import jax
import jax.numpy as jnp
from jax import lax

C = 16
NX = 8
NY = 64
NZ = 512


def draw_volume(key, part):
    first, second, third = jax.random.split(jax.random.fold_in(key, 11), 3)
    channel_scale = jax.random.uniform(second, (C, 1, 1, 1), jnp.float32, 0.5, 2.0)
    offset = jax.random.uniform(third, (C, 1, 1, 1), jnp.float32, -1.0, 1.0)
    ramp = jnp.arange(NX, dtype=jnp.float32) / max(NX - 1, 1)
    rising = jnp.power(3.0, ramp).reshape(1, NX, 1, 1)
    noise = jnp.clip(jax.random.normal(first, (C, NX, NY, NZ), jnp.float32), -4.0, 4.0)
    return channel_scale * rising * noise + offset


def draw_cotangent(key, part):
    first, second, third = jax.random.split(jax.random.fold_in(key, 23), 3)
    ramp = jnp.arange(NX, dtype=jnp.float32) / max(NX - 1, 1)
    tilt = (0.5 + ramp).reshape(1, NX, 1, 1)
    signs = jnp.where(jax.random.uniform(third, (C, 1, 1, 1), jnp.float32) < 0.5, -1.0, 1.0)
    magnitude = jax.random.uniform(second, (C, 1, 1, 1), jnp.float32, 0.4, 1.0)
    noise = jnp.clip(jax.random.normal(first, (C, NX, NY, NZ), jnp.float32), -4.0, 4.0)
    return noise + signs * magnitude * tilt


def gaussian(own_key, dims, deviation, most, kind=jnp.bfloat16):
    drawn = deviation * jax.random.normal(own_key, dims, jnp.float32)
    return jnp.clip(drawn, min=-most, max=most).astype(kind)


def setup_inputs(seed: int = 0) -> dict:
    key_list = jax.random.split(jax.random.key(seed), 6)
    volume = draw_volume(jax.random.fold_in(key_list[5], 71), 0)
    weight = gaussian(key_list[1], (C, C, 3, 3, 3), (C * 27) ** -0.5, 0.3125, jnp.float32)
    gamma = jnp.clip(jax.random.uniform(key_list[2], (C,), jnp.float32, 0.5, 1.5), 0.5, 1.5)
    beta = jnp.clip(jax.random.uniform(key_list[3], (C,), jnp.float32, -0.5, 0.5), -0.5, 0.5)
    cotangent = draw_cotangent(jax.random.fold_in(key_list[5], 71), 0)
    return {"volume": volume, "weight": weight, "gamma": gamma, "beta": beta, "cotangent": cotangent}


def mix(kernel, slab):
    return jnp.einsum('oi,ixyz->oxyz', kernel, slab, precision=lax.Precision.HIGHEST)

def reference(volume, weight, gamma, beta, cotangent):
    count = float(NX * NY * NZ)
    conv = jnp.zeros(volume.shape, jnp.float32)
    for a in range(3):
        for b in range(3):
            for c in range(3):
                conv = conv + mix(weight[:, :, a, b, c], jnp.roll(volume, (1 - a, 1 - b, 1 - c), axis=(1, 2, 3)))
    mean = lax.optimization_barrier(jnp.sum(conv, axis=(1, 2, 3))) / count
    centred = conv - mean[:, None, None, None]
    var = lax.optimization_barrier(jnp.sum(centred * centred, axis=(1, 2, 3))) / count
    rstd = lax.rsqrt(var + 1e-05)
    normed = centred * rstd[:, None, None, None]
    act = gamma[:, None, None, None] * normed + beta[:, None, None, None]
    sig = jax.nn.sigmoid(act)
    act_grad = cotangent * sig * (1.0 + act * (1.0 - sig))
    gamma_grad = lax.optimization_barrier(jnp.sum(act_grad * normed, axis=(1, 2, 3)))
    beta_grad = lax.optimization_barrier(jnp.sum(act_grad, axis=(1, 2, 3)))
    scale = (gamma * rstd)[:, None, None, None]
    conv_grad = scale * (act_grad - (beta_grad / count)[:, None, None, None] - normed * (gamma_grad / count)[:, None, None, None])
    pieces = []
    input_grad = jnp.zeros(volume.shape, jnp.float32)
    for a in range(3):
        for b in range(3):
            for c in range(3):
                slab = jnp.roll(volume, (1 - a, 1 - b, 1 - c), axis=(1, 2, 3))
                pieces.append(jnp.einsum('oxyz,ixyz->oi', conv_grad, slab, precision=lax.Precision.HIGHEST))
                input_grad = input_grad + mix(weight[:, :, a, b, c].T, jnp.roll(conv_grad, (a - 1, b - 1, c - 1), axis=(1, 2, 3)))
    weight_grad = jnp.stack(pieces, axis=2).reshape(C, C, 3, 3, 3)
    return (input_grad, weight_grad, gamma_grad, beta_grad)
```

```python
import functools

import jax
import jax.numpy as jnp
from jax import lax
from jax.experimental import pallas as pl
from jax.experimental.pallas import tpu as pltpu
from jax.sharding import PartitionSpec as P

AXES = ("gx", "gy", "gz")
F32, BF16 = jnp.float32, jnp.bfloat16


def call(body, outs, scratch=(), name=None):
    return pl.pallas_call(
        body,
        out_shape=[jax.ShapeDtypeStruct(shape, kind) for shape, kind in outs],
        scratch_shapes=list(scratch),
        name=name,
        compiler_params=pltpu.CompilerParams(vmem_limit_bytes=60 * 2**20),
    )


def turns(count):
    forward = [(i, (i + 1) % count) for i in range(count)]
    return forward, [(target, source) for source, target in forward]


def joint(first, second, wide):
    return [(a * wide + b, c * wide + d) for a, c in first for b, d in second]


def faces(store, field, x, y, size_x, size_y, value):
    grid, x_face, y_low, y_high, xy_low, xy_high = store
    grid[field, x, y] = value
    sides = ([0] if x == 0 else []) + ([1] if x == size_x - 1 else [])
    for side in sides:
        x_face[side, field, y] = value
    for edge, line, corner in ((0, y_low, xy_low), (size_y - 1, y_high, xy_high)):
        if y == edge:
            line[field, x] = value
            for side in sides:
                corner[side, field] = value


def face_shapes(fields, dims):
    size_x, size_y, chans, size_z = dims
    return [
        ((fields, size_x, size_y, chans, size_z), F32),
        ((2, fields, size_y, chans, size_z), F32),
        ((fields, size_x, chans, size_z), F32),
        ((fields, size_x, chans, size_z), F32),
        ((2, fields, chans, size_z), F32),
        ((2, fields, chans, size_z), F32),
    ]


def split_faces(dims, volume, *store):
    size_x, size_y, chans, size_z = dims
    for x in range(size_x):
        for y in range(size_y):
            value = volume[pl.ds(x * size_y + y, chans, stride=size_x * size_y), :]
            faces(store, 0, x, y, size_x, size_y, value)


def pad_kernel(fields, dims, grid, x_face, y_low, y_high, xy_low, xy_high, padded, first, last):
    size_x, size_y, chans, size_z = dims
    wide = size_y + 2
    pairs = padded.shape[1]
    group = 128 // chans
    for field in range(fields):
        for x in range(size_x):
            padded[field, pl.ds((x + 1) * wide + 1, size_y)] = grid[field, x]
            padded[field, (x + 1) * wide] = y_low[field, x]
            padded[field, (x + 1) * wide + size_y + 1] = y_high[field, x]
        for side, row in ((1, 0), (0, size_x + 1)):
            padded[field, pl.ds(row * wide + 1, size_y)] = x_face[side, field]
            padded[field, row * wide] = xy_low[side, field]
            padded[field, row * wide + size_y + 1] = xy_high[side, field]
        used = (size_x + 2) * wide
        if pairs > used:
            padded[field, pl.ds(used, pairs - used)] = jnp.zeros((pairs - used, chans, size_z), F32)
        rows = first.shape[0] // fields
        for at in range(pairs // group):
            block = padded[field, pl.ds(at * group, group)].reshape(group * chans, size_z)
            turned = block.T
            first[field * rows + at : field * rows + at + 1] = turned[:1]
            last[field * rows + at : field * rows + at + 1] = turned[size_z - 1 :]


def exchange(fields, dims, grid, x_face, y_low, y_high, xy_low, xy_high):
    size_x, size_y, chans, size_z = dims
    count_x, count_y, count_z = (lax.axis_size(axis) for axis in AXES)
    up_x, down_x = turns(count_x)
    up_y, down_y = turns(count_y)
    up_z, down_z = turns(count_z)

    def over_x(pieces, second, axes):
        def pairs(first):
            return first if second is None else joint(first, second, count_y)

        if count_x == 2:
            return lax.ppermute(pieces, axes, pairs(up_x))
        return jnp.stack(
            [lax.ppermute(pieces[0], axes, pairs(down_x)), lax.ppermute(pieces[1], axes, pairs(up_x))]
        )

    x_halo = over_x(x_face, None, "gx")
    low = lax.ppermute(y_high, "gy", up_y)
    high = lax.ppermute(y_low, "gy", down_y)
    xy_low_halo = over_x(xy_high, up_y, ("gx", "gy"))
    xy_high_halo = over_x(xy_low, down_y, ("gx", "gy"))
    group = 128 // chans
    groups = -(-(size_x + 2) * (size_y + 2) // group)
    rows = -(-groups // 8) * 8
    padded, first, last = call(
        functools.partial(pad_kernel, fields, dims),
        [
            ((fields, groups * group, chans, size_z), F32),
            ((fields * rows, 128), F32),
            ((fields * rows, 128), F32),
        ],
        name="pad_faces",
    )(grid, x_halo, low, high, xy_low_halo, xy_high_halo)
    before = lax.ppermute(last, "gz", up_z)
    after = lax.ppermute(first, "gz", down_z)
    return padded, before, after


def halo_block(before, after, row, size_z):
    rows = jnp.concatenate(
        [
            after[pl.ds(row, 1), :],
            jnp.zeros((size_z - 2, 128), F32),
            before[pl.ds(row, 1), :],
        ],
        axis=0,
    )
    return rows.T


def put_shifts(pair, value, edge, high, low):
    chans, size_z = value.shape
    lane = lax.broadcasted_iota(jnp.int32, value.shape, 1)
    left = pltpu.roll(jnp.where(lane == size_z - 1, edge, value), 1, 1)
    right = pltpu.roll(jnp.where(lane == 0, edge, value), size_z - 1, 1)
    for tap, part in enumerate((left, value, right)):
        top = part.astype(BF16)
        high[pair, tap * chans : (tap + 1) * chans] = top
        low[pair, tap * chans : (tap + 1) * chans] = (part - top.astype(F32)).astype(BF16)


def window(source, x, y, wide, count):
    columns = []
    for at in range(count):
        rows = []
        for first in range(3):
            block = source[pl.ds((x + first) * wide + y + at, 3)]
            rows.append(block.reshape(3 * block.shape[1], block.shape[2]))
        columns.append(jnp.concatenate(rows, axis=0))
    return jnp.concatenate(columns, axis=1)


def product(both, top, high, low, x, y, wide, count):
    chans = top.shape[0]
    wide_part = jnp.dot(both, window(high, x, y, wide, count), preferred_element_type=F32)
    thin_part = jnp.dot(top, window(low, x, y, wide, count), preferred_element_type=F32)
    return wide_part[:chans] + (wide_part[chans:] + thin_part)


def conv_kernel(dims, padded, before, after, both, top, conv, high, low, stats):
    size_x, size_y, chans, size_z = dims
    wide = size_y + 2
    group = 128 // chans

    def shifts(at, _):
        edges = halo_block(before, after, at, size_z)
        for one in range(group):
            pair = at * group + one
            edge = edges[one * chans : (one + 1) * chans]
            put_shifts(pair, padded[0, pair], edge, high, low)
        return 0

    lax.fori_loop(0, padded.shape[1] // group, shifts, 0)
    width = 2
    both_now, top_now = both[...], top[...]

    def step(at, carry):
        x, y = at // (size_y // width), (at % (size_y // width)) * width
        out = product(both_now, top_now, high, low, x, y, wide, width)
        total, source = carry
        for one in range(width):
            part = out[:, one * size_z : (one + 1) * size_z]
            conv[x, y + one] = part
            total = total + part
            source = source + padded[0, (x + 1) * wide + 1 + y + one]
        return total, source

    zero = jnp.zeros((chans, size_z), F32)
    total, source = lax.fori_loop(0, size_x * size_y // width, step, (zero, zero))
    sums = jnp.sum(total, axis=1, keepdims=True)
    centre = sums * (1.0 / (size_x * size_y * size_z))

    def spread(x, squares):
        for y in range(size_y):
            away = conv[x, y] - centre
            squares = squares + away * away
        return squares

    squares = lax.fori_loop(0, size_x, spread, zero)
    lane = lax.broadcasted_iota(jnp.int32, (chans, 128), 1)
    table = jnp.where(
        lane == 0,
        sums,
        jnp.where(
            lane == 1,
            jnp.sum(squares, axis=1, keepdims=True),
            jnp.where(lane == 2, jnp.sum(source, axis=1, keepdims=True), 0.0),
        ),
    )
    full = jnp.concatenate([table, jnp.zeros((128 - chans, 128), F32)], axis=0).T
    row = full[0:1] + pltpu.roll(full[1:2], chans, 1) + pltpu.roll(full[2:3], 2 * chans, 1)
    stats[...] = jnp.broadcast_to(row, stats.shape)


def act_kernel(dims, count, conv, cotangent, high, low, stats, gamma, beta, *outs):
    size_x, size_y, chans, size_z = dims
    store, sums, scales = outs[:6], outs[6], outs[7]
    local = float(size_x * size_y * size_z)
    wide = size_y + 2
    rows = stats[...]
    lane = lax.broadcasted_iota(jnp.int32, rows.shape, 1)
    mean_row = jnp.sum(rows, axis=0, keepdims=True) * (1.0 / count)
    away = jnp.where(lane < chans, rows * (1.0 / local) - mean_row, 0.0)
    spread_row = jnp.sum(away * away, axis=0, keepdims=True) * (local / count)
    var_row = mean_row + pltpu.roll(spread_row, chans, 1)
    rstd_row = lax.rsqrt(var_row + 1e-05)
    table = jnp.concatenate([mean_row, rstd_row, jnp.zeros((126, 128), F32)], axis=0).T
    mean = table[:chans, 0:1]
    rstd = table[chans : 2 * chans, 1:2]
    level = table[2 * chans : 3 * chans, 0:1]
    gain, shift = gamma[...], beta[...]
    scales[...] = jnp.broadcast_to(gain * rstd, scales.shape)
    gamma_sum = jnp.zeros((chans, size_z), F32)
    beta_sum = jnp.zeros((chans, size_z), F32)
    for x in range(size_x):
        for y in range(size_y):
            normed = (conv[x, y] - mean) * rstd
            act = gain * normed + shift
            sig = 1.0 / (1.0 + jnp.exp(-act))
            pull = cotangent[pl.ds(x * size_y + y, chans, stride=size_x * size_y), :]
            grad = pull * sig * (1.0 + act * (1.0 - sig))
            gamma_sum = gamma_sum + grad * normed
            beta_sum = beta_sum + grad
            faces(store, 0, x, y, size_x, size_y, grad)
            faces(store, 1, x, y, size_x, size_y, normed)
    gamma_part = jnp.sum(gamma_sum, axis=1, keepdims=True)
    beta_part = jnp.sum(beta_sum, axis=1, keepdims=True)
    centre = beta_part * (1.0 / local)
    grid = store[0]
    width = 4
    ones = jnp.ones((chans, size_z), BF16)

    def step(at, total):
        x, y = at // (size_y // width), (at % (size_y // width)) * width
        columns = []
        for one in range(width):
            grad = grid[0, x, y + one] - centre
            normed = grid[1, x, y + one]
            grad_top = grad.astype(BF16)
            normed_top = normed.astype(BF16)
            columns.append(
                jnp.concatenate(
                    [
                        grad_top,
                        (grad - grad_top.astype(F32)).astype(BF16),
                        normed_top,
                        (normed - normed_top.astype(F32)).astype(BF16),
                        ones,
                    ],
                    axis=0,
                )
            )
        right = jnp.concatenate(columns, axis=1)
        dims_in = (((1,), (1,)), ((), ()))
        for part in (high, low):
            left = window(part, x, y, wide, width)
            total = total + lax.dot_general(left, right, dims_in, preferred_element_type=F32)
        return total

    taps = 27 * chans
    total = lax.fori_loop(
        0, size_x * size_y // width, step, jnp.zeros((taps, 5 * chans), F32)
    )
    tall = -(-taps // 128) * 128
    levels = jnp.concatenate([level] * 27, axis=0)
    spare = 128 - 5 * chans
    side = jnp.concatenate([total, jnp.broadcast_to(levels, (taps, spare))], axis=1)
    side = jnp.concatenate([side, jnp.zeros((tall - taps, 128), F32)], axis=0)
    turned = jnp.concatenate(
        [side[at : at + 128].T for at in range(0, tall, 128)], axis=1
    )
    drift = turned[4 * chans : 4 * chans + 1] - local * turned[5 * chans : 5 * chans + 1]
    main = turned[:chans] + turned[chans : 2 * chans] + centre * drift
    other = turned[2 * chans : 3 * chans] + turned[3 * chans : 4 * chans]
    lane = lax.broadcasted_iota(jnp.int32, main.shape, 1)
    main = jnp.where(lane == taps, gamma_part, jnp.where(lane == taps + 1, beta_part, main))
    sums[0:chans] = main
    sums[chans : 2 * chans] = other


def grad_kernel(dims, count, padded, before, after, sums, scales, both, top, out, weight_grad, high, low):
    size_x, size_y, chans, size_z = dims
    wide = size_y + 2
    group = 128 // chans
    taps = 27 * chans
    scale = scales[...]
    main, other = sums[0:chans], sums[chans : 2 * chans]
    gamma_mean = main[:, taps : taps + 1] * (1.0 / count)
    beta_mean = main[:, taps + 1 : taps + 2] * (1.0 / count)
    weight_grad[...] = scale[:, 0:1] * (main - gamma_mean * other)
    gamma_wide = jnp.broadcast_to(gamma_mean, (chans, size_z))
    beta_wide = jnp.broadcast_to(beta_mean, (chans, size_z))
    rows = before.shape[0] // 2

    def mixed(grad, normed):
        return scale * (grad - beta_wide - normed * gamma_wide)

    def shifts(at, _):
        edge_grad = halo_block(before, after, at, size_z)
        edge_normed = halo_block(before, after, rows + at, size_z)
        for one in range(group):
            pair = at * group + one
            part = slice(one * chans, (one + 1) * chans)
            value = mixed(padded[0, pair], padded[1, pair])
            edge = mixed(edge_grad[part], edge_normed[part])
            put_shifts(pair, value, edge, high, low)
        return 0

    lax.fori_loop(0, padded.shape[1] // group, shifts, 0)
    width = 2
    both_now, top_now = both[...], top[...]
    stride = size_x * size_y

    def step(at, _):
        x, y = at // (size_y // width), (at % (size_y // width)) * width
        value = product(both_now, top_now, high, low, x, y, wide, width)
        for one in range(width):
            out[pl.ds(x * size_y + y + one, chans, stride=stride), :] = value[
                :, one * size_z : (one + 1) * size_z
            ]
        return 0

    lax.fori_loop(0, size_x * size_y // width, step, 0)


def total_over(value):
    for axis in ("gz", "gx", "gy"):
        count = lax.axis_size(axis)
        if count & (count - 1):
            value = lax.psum(value, axis)
            continue
        step = 1
        while step < count:
            value = value + lax.ppermute(value, axis, [(i, i ^ step) for i in range(count)])
            step *= 2
    return value


def two_parts(table):
    top = lax.reduce_precision(table, 8, 7)
    rest = (table - top).astype(BF16)
    top = top.astype(BF16)
    return jnp.concatenate([top, rest], axis=0), top


def shards(volume, weight, gamma, beta, cotangent):
    chans, size_x, size_y, size_z = volume.shape
    devices = 1
    for axis in AXES:
        devices *= lax.axis_size(axis)
    dims = (size_x, size_y, chans, size_z)
    count = float(size_x * size_y * size_z * devices)
    taps = 27 * chans
    tall = -(-taps // 128) * 128
    flat = (chans * size_x * size_y, size_z)
    store = call(functools.partial(split_faces, dims), face_shapes(1, dims), name="faces")(
        volume.reshape(flat)
    )
    padded, before, after = exchange(1, dims, *store)
    both, top = two_parts(weight.transpose(0, 2, 3, 4, 1).reshape(chans, taps))
    back = weight[:, :, ::-1, ::-1, ::-1].transpose(1, 2, 3, 4, 0).reshape(chans, taps)
    back_both, back_top = two_parts(back)
    pairs = padded.shape[1]
    conv, high, low, stats = call(
        functools.partial(conv_kernel, dims),
        [
            ((size_x, size_y, chans, size_z), F32),
            ((pairs, 3 * chans, size_z), BF16),
            ((pairs, 3 * chans, size_z), BF16),
            ((devices, 128), F32),
        ],
        name="conv",
    )(padded, before, after, both, top)
    stats = lax.all_to_all(stats, AXES, 0, 0, tiled=True)
    *store, sums, scales = call(
        functools.partial(act_kernel, dims, count),
        face_shapes(2, dims) + [((2 * chans, tall), F32), ((chans, size_z), F32)],
        name="act",
    )(conv, cotangent.reshape(flat), high, low, stats, gamma[:, None], beta[:, None])
    padded, before, after = exchange(2, dims, *store)
    sums = total_over(sums)
    input_grad, weight_grad = call(
        functools.partial(grad_kernel, dims, count),
        [(flat, F32), ((chans, tall), F32)],
        scratch=[
            pltpu.VMEM((pairs, 3 * chans, size_z), BF16),
            pltpu.VMEM((pairs, 3 * chans, size_z), BF16),
        ],
        name="grads",
    )(padded, before, after, sums, scales, back_both, back_top)
    weight_grad = weight_grad[:, :taps].reshape(chans, 3, 3, 3, chans).transpose(0, 4, 1, 2, 3)
    return (
        input_grad.reshape(volume.shape),
        weight_grad,
        sums[:chans, taps],
        sums[:chans, taps + 1],
    )


def solution(mesh):
    return jax.shard_map(
        shards,
        mesh=mesh,
        in_specs=(P(None, "gx", "gy", "gz"), P(), P(), P(), P(None, "gx", "gy", "gz")),
        out_specs=(P(None, "gx", "gy", "gz"), P(), P(), P()),
        check_vma=False,
    )
```

```python
import functools
import math

import jax
import jax.numpy as jnp
from jax import lax
from jax.experimental import pallas as pl
from jax.experimental.pallas import tpu as pltpu
from jax.sharding import PartitionSpec as P

AXES = ("gx", "gy", "gz")
F32, BF16 = jnp.float32, jnp.bfloat16


def call(body, outs, scratch=(), name=None, last=False):
    run = pl.pallas_call(
        body,
        out_shape=[
            jax.ShapeDtypeStruct(shape, kind) if last else pltpu.VMEM(shape, kind)
            for shape, kind in outs
        ],
        scratch_shapes=list(scratch),
        name=name,
        compiler_params=pltpu.CompilerParams(vmem_limit_bytes=16 * 2**20),
    )

    def onchip(*args):
        return run(*[pltpu.with_memory_space_constraint(arg, pltpu.VMEM) for arg in args])

    return onchip


def turns(count):
    forward = [(i, (i + 1) % count) for i in range(count)]
    return forward, [(target, source) for source, target in forward]


def joint(first, second, wide):
    return [(a * wide + b, c * wide + d) for a, c in first for b, d in second]


def faces(store, field, x, y, size_x, size_y, value):
    grid, x_face, y_low, y_high, xy_low, xy_high = store
    grid[field, x, y] = value
    sides = ([0] if x == 0 else []) + ([1] if x == size_x - 1 else [])
    for side in sides:
        x_face[side, field, y] = value
    for edge, line, corner in ((0, y_low, xy_low), (size_y - 1, y_high, xy_high)):
        if y == edge:
            line[field, x] = value
            for side in sides:
                corner[side, field] = value


def face_shapes(fields, dims):
    size_x, size_y, chans, size_z = dims
    return [
        ((fields, size_x, size_y, chans, size_z), F32),
        ((2, fields, size_y, chans, size_z), F32),
        ((fields, size_x, chans, size_z), F32),
        ((fields, size_x, chans, size_z), F32),
        ((2, fields, chans, size_z), F32),
        ((2, fields, chans, size_z), F32),
    ]


def split_faces(dims, volume, *store):
    size_x, size_y, chans, size_z = dims
    for x in range(size_x):
        for y in range(size_y):
            value = volume[pl.ds(x * size_y + y, chans, stride=size_x * size_y), :]
            faces(store, 0, x, y, size_x, size_y, value)


def pad_kernel(fields, dims, grid, x_face, y_low, y_high, xy_low, xy_high, padded, first, last):
    size_x, size_y, chans, size_z = dims
    wide = size_y + 2
    pairs = padded.shape[1]
    group = 128 // chans
    for field in range(fields):
        for x in range(size_x):
            padded[field, pl.ds((x + 1) * wide + 1, size_y)] = grid[field, x]
            padded[field, (x + 1) * wide] = y_low[field, x]
            padded[field, (x + 1) * wide + size_y + 1] = y_high[field, x]
        for side, row in ((1, 0), (0, size_x + 1)):
            padded[field, pl.ds(row * wide + 1, size_y)] = x_face[side, field]
            padded[field, row * wide] = xy_low[side, field]
            padded[field, row * wide + size_y + 1] = xy_high[side, field]
        used = (size_x + 2) * wide
        if pairs > used:
            padded[field, pl.ds(used, pairs - used)] = jnp.zeros((pairs - used, chans, size_z), F32)
        rows = first.shape[0] // fields
        for at in range(pairs // group):
            block = padded[field, pl.ds(at * group, group)].reshape(group * chans, size_z)
            turned = block.T
            first[field * rows + at : field * rows + at + 1] = turned[:1]
            last[field * rows + at : field * rows + at + 1] = turned[size_z - 1 :]


def exchange(fields, dims, grid, x_face, y_low, y_high, xy_low, xy_high):
    size_x, size_y, chans, size_z = dims
    count_x, count_y, count_z = (lax.axis_size(axis) for axis in AXES)
    up_x, down_x = turns(count_x)
    up_y, down_y = turns(count_y)
    up_z, down_z = turns(count_z)

    def over_x(pieces, second, axes):
        def pairs(first):
            return first if second is None else joint(first, second, count_y)

        if count_x == 2:
            return lax.ppermute(pieces, axes, pairs(up_x))
        return jnp.stack(
            [lax.ppermute(pieces[0], axes, pairs(down_x)), lax.ppermute(pieces[1], axes, pairs(up_x))]
        )

    x_halo = over_x(x_face, None, "gx")
    low = lax.ppermute(y_high, "gy", up_y)
    high = lax.ppermute(y_low, "gy", down_y)
    xy_low_halo = over_x(xy_high, up_y, ("gx", "gy"))
    xy_high_halo = over_x(xy_low, down_y, ("gx", "gy"))
    group = 128 // chans
    groups = -(-(size_x + 2) * (size_y + 2) // group)
    rows = -(-groups // 8) * 8
    padded, first, last = call(
        functools.partial(pad_kernel, fields, dims),
        [
            ((fields, groups * group, chans, size_z), F32),
            ((fields * rows, 128), F32),
            ((fields * rows, 128), F32),
        ],
        name="pad_faces",
    )(grid, x_halo, low, high, xy_low_halo, xy_high_halo)
    before = lax.ppermute(last, "gz", up_z)
    after = lax.ppermute(first, "gz", down_z)
    return padded, before, after


def halo_block(before, after, row, size_z):
    rows = jnp.concatenate(
        [
            after[pl.ds(row, 1), :],
            jnp.zeros((size_z - 2, 128), F32),
            before[pl.ds(row, 1), :],
        ],
        axis=0,
    )
    return rows.T


def put_shifts(pair, value, edge, high, low):
    chans, size_z = value.shape
    lane = lax.broadcasted_iota(jnp.int32, value.shape, 1)
    left = pltpu.roll(jnp.where(lane == size_z - 1, edge, value), 1, 1)
    right = pltpu.roll(jnp.where(lane == 0, edge, value), size_z - 1, 1)
    for tap, part in enumerate((left, value, right)):
        top = part.astype(BF16)
        high[pair, tap * chans : (tap + 1) * chans] = top
        low[pair, tap * chans : (tap + 1) * chans] = (part - top.astype(F32)).astype(BF16)


def window(source, x, y, wide, count):
    columns = []
    for at in range(count):
        rows = []
        for first in range(3):
            block = source[pl.ds((x + first) * wide + y + at, 3)]
            rows.append(block.reshape(3 * block.shape[1], block.shape[2]))
        columns.append(jnp.concatenate(rows, axis=0))
    return jnp.concatenate(columns, axis=1)


def product(both, top, high, low, x, y, wide, count):
    chans = top.shape[0]
    wide_part = jnp.dot(both, window(high, x, y, wide, count), preferred_element_type=F32)
    thin_part = jnp.dot(top, window(low, x, y, wide, count), preferred_element_type=F32)
    return wide_part[:chans] + (wide_part[chans:] + thin_part)


def volume_shifts(padded, before, after, high, low):
    chans, size_z = padded.shape[2:]
    group = 128 // chans
    for at in range(padded.shape[1] // group):
        edges = halo_block(before, after, at, size_z)
        for one in range(group):
            pair = at * group + one
            edge = edges[one * chans : (one + 1) * chans]
            put_shifts(pair, padded[0, pair], edge, high, low)


def conv_kernel(dims, padded, before, after, both, top, conv, stats, high, low):
    size_x, size_y, chans, size_z = dims
    wide = size_y + 2
    volume_shifts(padded, before, after, high, low)
    width = math.gcd(size_y, 8)
    both_now, top_now = both[...], top[...]

    def step(at, carry):
        x, y = at // (size_y // width), (at % (size_y // width)) * width
        out = product(both_now, top_now, high, low, x, y, wide, width)
        total, source = carry
        for one in range(width):
            part = out[:, one * size_z : (one + 1) * size_z]
            conv[x, y + one] = part
            total = total + part
            source = source + padded[0, (x + 1) * wide + 1 + y + one]
        return total, source

    zero = jnp.zeros((chans, size_z), F32)
    total, source = lax.fori_loop(
        0, size_x * size_y // width, step, (zero, zero), unroll=True
    )
    sums = jnp.sum(total, axis=1, keepdims=True)
    centre = sums * (1.0 / (size_x * size_y * size_z))

    def spread(x, squares):
        for y in range(size_y):
            away = conv[x, y] - centre
            squares = squares + away * away
        return squares

    squares = lax.fori_loop(0, size_x, spread, zero, unroll=True)
    lane = lax.broadcasted_iota(jnp.int32, (chans, 128), 1)
    table = jnp.where(
        lane == 0,
        sums,
        jnp.where(
            lane == 1,
            jnp.sum(squares, axis=1, keepdims=True),
            jnp.where(lane == 2, jnp.sum(source, axis=1, keepdims=True), 0.0),
        ),
    )
    full = jnp.concatenate([table, jnp.zeros((128 - chans, 128), F32)], axis=0).T
    row = full[0:1] + pltpu.roll(full[1:2], chans, 1) + pltpu.roll(full[2:3], 2 * chans, 1)
    stats[...] = jnp.broadcast_to(row, stats.shape)


def act_kernel(dims, count, conv, cotangent, padded, before, after, stats, gamma, beta, *outs):
    size_x, size_y, chans, size_z = dims
    store, sums, scales, high, low = outs[:6], *outs[6:]
    volume_shifts(padded, before, after, high, low)
    local = float(size_x * size_y * size_z)
    wide = size_y + 2
    rows = stats[...]
    lane = lax.broadcasted_iota(jnp.int32, rows.shape, 1)
    mean_row = jnp.sum(rows, axis=0, keepdims=True) * (1.0 / count)
    away = jnp.where(lane < chans, rows * (1.0 / local) - mean_row, 0.0)
    spread_row = jnp.sum(away * away, axis=0, keepdims=True) * (local / count)
    var_row = mean_row + pltpu.roll(spread_row, chans, 1)
    rstd_row = lax.rsqrt(var_row + 1e-05)
    blank = jnp.zeros((1, 128 - chans), F32)
    gain_row = jnp.concatenate([gamma[...], blank], axis=1)
    shift_row = jnp.concatenate([beta[...], blank], axis=1)
    table = jnp.concatenate(
        [mean_row, rstd_row, gain_row, shift_row, jnp.zeros((124, 128), F32)], axis=0
    ).T
    mean = table[:chans, 0:1]
    rstd = table[chans : 2 * chans, 1:2]
    level = table[2 * chans : 3 * chans, 0:1]
    gain, shift = table[:chans, 2:3], table[:chans, 3:4]
    scales[...] = jnp.broadcast_to(gain * rstd, scales.shape)
    gamma_sum = jnp.zeros((chans, size_z), F32)
    beta_sum = jnp.zeros((chans, size_z), F32)
    for x in range(size_x):
        for y in range(size_y):
            normed = (conv[x, y] - mean) * rstd
            act = gain * normed + shift
            sig = 1.0 / (1.0 + jnp.exp(-act))
            pull = cotangent[pl.ds(x * size_y + y, chans, stride=size_x * size_y), :]
            grad = pull * sig * (1.0 + act * (1.0 - sig))
            gamma_sum = gamma_sum + grad * normed
            beta_sum = beta_sum + grad
            faces(store, 0, x, y, size_x, size_y, grad)
            faces(store, 1, x, y, size_x, size_y, normed)
    gamma_part = jnp.sum(gamma_sum, axis=1, keepdims=True)
    beta_part = jnp.sum(beta_sum, axis=1, keepdims=True)
    centre = beta_part * (1.0 / local)
    grid = store[0]
    width = 4
    ones = jnp.ones((chans, size_z), BF16)

    def step(at, total):
        x, y = at // (size_y // width), (at % (size_y // width)) * width
        columns = []
        for one in range(width):
            grad = grid[0, x, y + one] - centre
            normed = grid[1, x, y + one]
            grad_top = grad.astype(BF16)
            normed_top = normed.astype(BF16)
            columns.append(
                jnp.concatenate(
                    [
                        grad_top,
                        (grad - grad_top.astype(F32)).astype(BF16),
                        normed_top,
                        (normed - normed_top.astype(F32)).astype(BF16),
                        ones,
                    ],
                    axis=0,
                )
            )
        right = jnp.concatenate(columns, axis=1)
        dims_in = (((1,), (1,)), ((), ()))
        for part in (high, low):
            left = window(part, x, y, wide, width)
            total = total + lax.dot_general(left, right, dims_in, preferred_element_type=F32)
        return total

    taps = 27 * chans
    total = lax.fori_loop(
        0, size_x * size_y // width, step, jnp.zeros((taps, 5 * chans), F32), unroll=True
    )
    tall = -(-taps // 128) * 128
    levels = jnp.concatenate([level] * 27, axis=0)
    spare = 128 - 5 * chans
    side = jnp.concatenate([total, jnp.broadcast_to(levels, (taps, spare))], axis=1)
    side = jnp.concatenate([side, jnp.zeros((tall - taps, 128), F32)], axis=0)
    turned = jnp.concatenate(
        [side[at : at + 128].T for at in range(0, tall, 128)], axis=1
    )
    drift = turned[4 * chans : 4 * chans + 1] - local * turned[5 * chans : 5 * chans + 1]
    main = turned[:chans] + turned[chans : 2 * chans] + centre * drift
    other = turned[2 * chans : 3 * chans] + turned[3 * chans : 4 * chans]
    lane = lax.broadcasted_iota(jnp.int32, main.shape, 1)
    main = jnp.where(lane == taps, gamma_part, jnp.where(lane == taps + 1, beta_part, main))
    sums[0:chans] = main
    sums[chans : 2 * chans] = other


def grad_kernel(dims, count, padded, before, after, sums, scales, both, top, out, high, low):
    size_x, size_y, chans, size_z = dims
    wide = size_y + 2
    group = 128 // chans
    taps = 27 * chans
    scale = scales[...]
    main = sums[0:chans]
    gamma_mean = main[:, taps : taps + 1] * (1.0 / count)
    beta_mean = main[:, taps + 1 : taps + 2] * (1.0 / count)
    gamma_wide = jnp.broadcast_to(gamma_mean, (chans, size_z))
    beta_wide = jnp.broadcast_to(beta_mean, (chans, size_z))
    rows = before.shape[0] // 2

    def mixed(grad, normed):
        return scale * (grad - beta_wide - normed * gamma_wide)

    def shifts(at, _):
        edge_grad = halo_block(before, after, at, size_z)
        edge_normed = halo_block(before, after, rows + at, size_z)
        for one in range(group):
            pair = at * group + one
            part = slice(one * chans, (one + 1) * chans)
            value = mixed(padded[0, pair], padded[1, pair])
            edge = mixed(edge_grad[part], edge_normed[part])
            put_shifts(pair, value, edge, high, low)
        return 0

    lax.fori_loop(0, padded.shape[1] // group, shifts, 0, unroll=True)
    width = math.gcd(size_y, 8)
    both_now, top_now = both[...], top[...]
    stride = size_x * size_y

    def step(at, _):
        x, y = at // (size_y // width), (at % (size_y // width)) * width
        value = product(both_now, top_now, high, low, x, y, wide, width)
        for one in range(width):
            out[pl.ds(x * size_y + y + one, chans, stride=stride), :] = value[
                :, one * size_z : (one + 1) * size_z
            ]
        return 0

    lax.fori_loop(0, size_x * size_y // width, step, 0, unroll=True)


def total_over(value):
    for axis in ("gz", "gx", "gy"):
        count = lax.axis_size(axis)
        if count & (count - 1):
            value = lax.psum(value, axis)
            continue
        step = 1
        while step < count:
            value = value + lax.ppermute(value, axis, [(i, i ^ step) for i in range(count)])
            step *= 2
    return value


def two_parts(table):
    top = lax.reduce_precision(table, 8, 7)
    rest = (table - top).astype(BF16)
    top = top.astype(BF16)
    return jnp.concatenate([top, rest], axis=0), top


def shards(volume, weight, gamma, beta, cotangent):
    chans, size_x, size_y, size_z = volume.shape
    devices = 1
    for axis in AXES:
        devices *= lax.axis_size(axis)
    dims = (size_x, size_y, chans, size_z)
    count = float(size_x * size_y * size_z * devices)
    taps = 27 * chans
    tall = -(-taps // 128) * 128
    flat = (chans * size_x * size_y, size_z)
    store = call(functools.partial(split_faces, dims), face_shapes(1, dims), name="faces")(
        volume.reshape(flat)
    )
    padded, before, after = exchange(1, dims, *store)
    both, top = two_parts(weight.transpose(0, 2, 3, 4, 1).reshape(chans, taps))
    back = weight[:, :, ::-1, ::-1, ::-1].transpose(1, 2, 3, 4, 0).reshape(chans, taps)
    back_both, back_top = two_parts(back)
    pairs = padded.shape[1]
    shifted = [pltpu.VMEM((pairs, 3 * chans, size_z), BF16)] * 2
    conv, stats = call(
        functools.partial(conv_kernel, dims),
        [((size_x, size_y, chans, size_z), F32), ((devices, 128), F32)],
        scratch=shifted,
        name="conv",
    )(padded, before, after, both, top)
    stats = lax.all_to_all(stats, AXES, 0, 0, tiled=True)
    stats, back_both, back_top = lax.optimization_barrier((stats, back_both, back_top))
    *store, sums, scales = call(
        functools.partial(act_kernel, dims, count),
        face_shapes(2, dims) + [((2 * chans, tall), F32), ((chans, size_z), F32)],
        scratch=shifted,
        name="act",
    )(conv, cotangent.reshape(flat), padded, before, after, stats, gamma[None], beta[None])
    padded, before, after = exchange(2, dims, *store)
    sums = total_over(sums)
    main, other = sums[:chans, :taps], sums[chans:, :taps]
    gamma_grad, beta_grad = sums[:chans, taps], sums[:chans, taps + 1]
    weight_grad = scales[:, :1] * (main - (gamma_grad / count)[:, None] * other)
    weight_grad = weight_grad.reshape(chans, 3, 3, 3, chans).transpose(0, 4, 1, 2, 3)
    (input_grad,) = call(
        functools.partial(grad_kernel, dims, count),
        [(flat, F32)],
        scratch=shifted,
        name="grads",
        last=True,
    )(padded, before, after, sums, scales, back_both, back_top)
    return input_grad.reshape(volume.shape), weight_grad, gamma_grad, beta_grad


def solution(mesh):
    return jax.shard_map(
        shards,
        mesh=mesh,
        in_specs=(P(None, "gx", "gy", "gz"), P(), P(), P(), P(None, "gx", "gy", "gz")),
        out_specs=(P(None, "gx", "gy", "gz"), P(), P(), P()),
        check_vma=False,
    )
```

```python
import functools
import math

import jax
import jax.numpy as jnp
from jax import lax
from jax.experimental import pallas as pl
from jax.experimental.pallas import tpu as pltpu
from jax.sharding import PartitionSpec as P


AXES = ("gx", "gy", "gz")
F32, BF16 = jnp.float32, jnp.bfloat16


def call(body, outs, scratch=(), last=False, far=()):
    run = pl.pallas_call(
        body,
        out_shape=[
            jax.ShapeDtypeStruct(shape, kind) if last else pltpu.VMEM(shape, kind)
            for shape, kind in outs
        ],
        scratch_shapes=list(scratch),
        compiler_params=pltpu.CompilerParams(vmem_limit_bytes=16 * 2**20),
    )

    def onchip(*args):
        places = [pltpu.HBM if at in far else pltpu.VMEM for at in range(len(args))]
        return run(*map(pltpu.with_memory_space_constraint, args, places))

    return onchip


def turns(count):
    forward = [(i, (i + 1) % count) for i in range(count)]
    return forward, [(target, source) for source, target in forward]


def joint(first, second, wide):
    return [(a * wide + b, c * wide + d) for a, c in first for b, d in second]


def put(store, field, x, y, size_x, value):
    grid, x_face = store[:2]
    grid[field, x, y] = value
    sides = ([0] if x == 0 else []) + ([1] if x == size_x - 1 else [])
    for side in sides:
        x_face[side, field, y] = value


def put_lines(store, fields, size_x, size_y):
    grid, _, even_line, odd_line, even_corner, odd_corner = store
    even = lax.rem(lax.axis_index("gy"), 2) == 0
    for field in range(fields):
        for x in range(size_x):
            bottom, top = grid[field, x, 0], grid[field, x, size_y - 1]
            one, two = jnp.where(even, top, bottom), jnp.where(even, bottom, top)
            even_line[field, x] = one
            odd_line[field, x] = two
            sides = ([0] if x == 0 else []) + ([1] if x == size_x - 1 else [])
            for side in sides:
                even_corner[side, field] = one
                odd_corner[side, field] = two


def face_shapes(fields, dims):
    size_x, size_y, chans, size_z = dims
    return [
        ((fields, size_x, size_y, chans, size_z), F32),
        ((2, fields, size_y, chans, size_z), F32),
        ((fields, size_x, chans, size_z), F32),
        ((fields, size_x, chans, size_z), F32),
        ((2, fields, chans, size_z), F32),
        ((2, fields, chans, size_z), F32),
    ]


def split_faces(dims, volume, *store):
    size_x, size_y, chans, _ = dims
    for x in range(size_x):
        for y in range(size_y):
            value = volume[pl.ds(x * size_y + y, chans, stride=size_x * size_y), :]
            put(store, 0, x, y, size_x, value)
    put_lines(store, 1, size_x, size_y)


def pad_kernel(fields, dims, grid, x_face, one, two, one_corner, two_corner, padded, first, last):
    size_x, size_y, chans, size_z = dims
    even = lax.rem(lax.axis_index("gy"), 2) == 0

    def ends(first_part, second_part):
        return jnp.where(even, second_part, first_part), jnp.where(even, first_part, second_part)

    wide = size_y + 2
    pairs = padded.shape[1]
    group = 128 // chans
    for field in range(fields):
        for x in range(size_x):
            padded[field, pl.ds((x + 1) * wide + 1, size_y)] = grid[field, x]
            low, high = ends(one[field, x], two[field, x])
            padded[field, (x + 1) * wide] = low
            padded[field, (x + 1) * wide + size_y + 1] = high
        for side, row in ((1, 0), (0, size_x + 1)):
            padded[field, pl.ds(row * wide + 1, size_y)] = x_face[side, field]
            low, high = ends(one_corner[side, field], two_corner[side, field])
            padded[field, row * wide] = low
            padded[field, row * wide + size_y + 1] = high
        used = (size_x + 2) * wide
        if pairs > used:
            padded[field, pl.ds(used, pairs - used)] = jnp.zeros((pairs - used, chans, size_z), F32)
        rows = first.shape[0] // fields
        for at in range(pairs // group):
            block = padded[field, pl.ds(at * group, group)].reshape(group * chans, size_z)
            turned = block.T
            first[field * rows + at : field * rows + at + 1] = turned[:1]
            last[field * rows + at : field * rows + at + 1] = turned[size_z - 1 :]


def exchange(far, fields, dims, grid, x_face, one, two, one_corner, two_corner):
    size_x, size_y, chans, size_z = dims
    count_x, count_y, count_z = (lax.axis_size(axis) for axis in AXES)
    up_x, down_x = turns(count_x)
    assert count_y % 2 == 0
    one_y = [(i, i ^ 1) for i in range(count_y)]
    two_y = [(i, (((i + 1) ^ 1) - 1) % count_y) for i in range(count_y)]
    up_z, down_z = turns(count_z)

    def over_x(pieces, second, axes):
        def pairs(first):
            return first if second is None else joint(first, second, count_y)

        if count_x == 2:
            return lax.ppermute(pieces, axes, pairs(up_x))
        return jnp.stack(
            [lax.ppermute(pieces[0], axes, pairs(down_x)), lax.ppermute(pieces[1], axes, pairs(up_x))]
        )

    x_halo = over_x(x_face, None, "gx")
    two = lax.ppermute(two, "gy", two_y)
    one = lax.ppermute(one, "gy", one_y)
    two_corner = over_x(two_corner, two_y, ("gx", "gy"))
    one_corner = over_x(one_corner, one_y, ("gx", "gy"))
    group = 128 // chans
    groups = -(-(size_x + 2) * (size_y + 2) // group)
    rows = -(-groups // 8) * 8
    padded, first, last = call(
        functools.partial(pad_kernel, fields, dims),
        [
            ((fields, groups * group, chans, size_z), F32),
            ((fields * rows, 128), F32),
            ((fields * rows, 128), F32),
        ],
        far=range(1, 6) if far else (),
    )(grid, x_halo, one, two, one_corner, two_corner)
    before = lax.ppermute(last, "gz", up_z)
    after = lax.ppermute(first, "gz", down_z)
    return padded, before, after


def halo_block(before, after, row, size_z):
    rows = jnp.concatenate(
        [
            after[row : row + 1],
            jnp.zeros((size_z - 2, 128), F32),
            before[row : row + 1],
        ],
        axis=0,
    )
    return rows.T


def put_shifts(pair, value, edge, high, low):
    chans, size_z = value.shape
    lane = lax.broadcasted_iota(jnp.int32, value.shape, 1)
    left = pltpu.roll(jnp.where(lane == size_z - 1, edge, value), 1, 1)
    right = pltpu.roll(jnp.where(lane == 0, edge, value), size_z - 1, 1)
    for tap, part in enumerate((left, value, right)):
        top = part.astype(BF16)
        high[pair, tap * chans : (tap + 1) * chans] = top
        low[pair, tap * chans : (tap + 1) * chans] = (part - top.astype(F32)).astype(BF16)


def window(source, x, y, wide, count):
    columns = []
    for at in range(count):
        rows = []
        for first in range(3):
            block = source[pl.ds((x + first) * wide + y + at, 3)]
            rows.append(block.reshape(3 * block.shape[1], block.shape[2]))
        columns.append(jnp.concatenate(rows, axis=0))
    return jnp.concatenate(columns, axis=1)


def product(both, top, high, low, x, y, wide, count):
    chans = top.shape[0]
    wide_part = jnp.dot(both, window(high, x, y, wide, count), preferred_element_type=F32)
    thin_part = jnp.dot(top, window(low, x, y, wide, count), preferred_element_type=F32)
    return wide_part[:chans] + (wide_part[chans:] + thin_part)


def volume_shifts(padded, before, after, high, low):
    chans, size_z = padded.shape[2:]
    group = 128 // chans
    for at in range(padded.shape[1] // group):
        edges = halo_block(before[...], after[...], at, size_z)
        for one in range(group):
            pair = at * group + one
            edge = edges[one * chans : (one + 1) * chans]
            put_shifts(pair, padded[0, pair], edge, high, low)


def conv_kernel(dims, padded, before, after, both, top, cotangent, *outs):
    size_x, size_y, chans, size_z = dims
    store, stats, high, low = outs[:6], *outs[6:]
    grid = store[0]
    wide = size_y + 2
    for x in range(size_x):
        for y in range(size_y):
            pull = cotangent[pl.ds(x * size_y + y, chans, stride=size_x * size_y), :]
            put(store, 0, x, y, size_x, pull)
    volume_shifts(padded, before, after, high, low)
    width = math.gcd(size_y, 8)
    both_now, top_now = both[...], top[...]

    zero = jnp.zeros((chans, size_z), F32)
    total, source = zero, zero
    for x in range(size_x):
        for y in range(0, size_y, width):
            out = product(both_now, top_now, high, low, x, y, wide, width)
            for one in range(width):
                part = out[:, one * size_z : (one + 1) * size_z]
                put(store, 1, x, y + one, size_x, part)
                total = total + part
                source = source + padded[0, (x + 1) * wide + 1 + y + one]
    put_lines(store, 2, size_x, size_y)
    sums = jnp.sum(total, axis=1, keepdims=True)
    centre = sums * (1.0 / (size_x * size_y * size_z))

    def spread(x, squares):
        for y in range(size_y):
            away = grid[1, x, y] - centre
            squares = squares + away * away
        return squares

    squares = lax.fori_loop(0, size_x, spread, zero, unroll=True)
    lane = lax.broadcasted_iota(jnp.int32, (chans, 128), 1)
    table = jnp.where(
        lane == 0,
        sums,
        jnp.where(
            lane == 1,
            jnp.sum(squares, axis=1, keepdims=True),
            jnp.where(lane == 2, jnp.sum(source, axis=1, keepdims=True), 0.0),
        ),
    )
    full = jnp.concatenate([table, jnp.zeros((128 - chans, 128), F32)], axis=0).T
    row = full[0:1] + pltpu.roll(full[1:2], chans, 1) + pltpu.roll(full[2:3], 2 * chans, 1)
    stats[...] = jnp.broadcast_to(row, stats.shape)


def slope(pull, conv, mean, rstd, gain, shift):
    normed = (conv - mean) * rstd
    act = gain * normed + shift
    sig = 1.0 / (1.0 + jnp.exp(-act))
    return pull * sig * (1.0 + act * (1.0 - sig)), normed


def act_kernel(
    dims, count, given, padded, before, after, stats, gamma, beta, *outs
):
    size_x, size_y, chans, size_z = dims
    keep, send, scales, high, low, grid = outs
    volume_shifts(padded, before, after, high, low)
    local = float(size_x * size_y * size_z)
    wide = size_y + 2
    rows = stats[...]
    lane = lax.broadcasted_iota(jnp.int32, rows.shape, 1)
    mean_row = jnp.sum(rows, axis=0, keepdims=True) * (1.0 / count)
    away = jnp.where(lane < chans, rows * (1.0 / local) - mean_row, 0.0)
    spread_row = jnp.sum(away * away, axis=0, keepdims=True) * (local / count)
    var_row = mean_row + pltpu.roll(spread_row, chans, 1)
    rstd_row = lax.rsqrt(var_row + 1e-05)
    blank = jnp.zeros((1, 128 - chans), F32)
    gain_row = jnp.concatenate([gamma[...], blank], axis=1)
    shift_row = jnp.concatenate([beta[...], blank], axis=1)
    table = jnp.concatenate(
        [mean_row, rstd_row, gain_row, shift_row, jnp.zeros((124, 128), F32)], axis=0
    ).T
    mean = table[:chans, 0:1]
    rstd = table[chans : 2 * chans, 1:2]
    level = table[2 * chans : 3 * chans, 0:1]
    gain, shift = table[:chans, 2:3], table[:chans, 3:4]
    scales[0:chans] = table[:chans]
    scales[chans : 2 * chans] = table[chans : 2 * chans]
    gamma_sum = jnp.zeros((chans, size_z), F32)
    beta_sum = jnp.zeros((chans, size_z), F32)
    for x in range(size_x):
        for y in range(size_y):
            grad, normed = slope(given[0, x, y], given[1, x, y], mean, rstd, gain, shift)
            gamma_sum = gamma_sum + grad * normed
            beta_sum = beta_sum + grad
            grid[0, x, y] = grad
            grid[1, x, y] = normed
    gamma_part = jnp.sum(gamma_sum, axis=1, keepdims=True)
    beta_part = jnp.sum(beta_sum, axis=1, keepdims=True)
    centre = beta_part * (1.0 / local)
    width = 4
    ones = jnp.ones((chans, size_z), BF16)

    def step(at, total):
        x, y = at // (size_y // width), (at % (size_y // width)) * width
        columns = []
        for one in range(width):
            grad = grid[0, x, y + one] - centre
            normed = grid[1, x, y + one]
            grad_top = grad.astype(BF16)
            normed_top = normed.astype(BF16)
            columns.append(
                jnp.concatenate(
                    [
                        grad_top,
                        (grad - grad_top.astype(F32)).astype(BF16),
                        normed_top,
                        (normed - normed_top.astype(F32)).astype(BF16),
                        ones,
                    ],
                    axis=0,
                )
            )
        right = jnp.concatenate(columns, axis=1)
        dims_in = (((1,), (1,)), ((), ()))
        for part in (high, low):
            left = window(part, x, y, wide, width)
            total = total + lax.dot_general(left, right, dims_in, preferred_element_type=F32)
        return total

    taps = 27 * chans
    total = lax.fori_loop(
        0, size_x * size_y // width, step, jnp.zeros((taps, 5 * chans), F32), unroll=True
    )
    tall = -(-taps // 128) * 128
    levels = jnp.concatenate([level] * 27, axis=0)
    spare = 128 - 5 * chans
    side = jnp.concatenate([total, jnp.broadcast_to(levels, (taps, spare))], axis=1)
    side = jnp.concatenate([side, jnp.zeros((tall - taps, 128), F32)], axis=0)
    turned = jnp.concatenate(
        [side[at : at + 128].T for at in range(0, tall, 128)], axis=1
    )
    drift = turned[4 * chans : 4 * chans + 1] - local * turned[5 * chans : 5 * chans + 1]
    main = turned[:chans] + turned[chans : 2 * chans] + centre * drift
    other = turned[2 * chans : 3 * chans] + turned[3 * chans : 4 * chans]
    lane = lax.broadcasted_iota(jnp.int32, main.shape, 1)
    main = jnp.where(lane == taps, gamma_part, jnp.where(lane == taps + 1, beta_part, main))
    even = lax.rem(lax.axis_index("gz"), 2) == 0
    keep[...] = jnp.where(even, main, other)
    send[...] = jnp.where(even, other, main)


def along(row, chans):
    lane = lax.broadcasted_iota(jnp.int32, row.shape, 1)
    row = jnp.where(lane < chans, row, 0.0)
    step = chans
    while step < 128:
        row = row + pltpu.roll(row, step, 1)
        step *= 2
    return row


def grad_kernel(dims, count, padded, before, after, part, other, scales, both, top, *outs):
    size_x, size_y, chans, size_z = dims
    wide = size_y + 2
    group = 128 // chans
    taps = 27 * chans
    rows = before.shape[0] // 2
    even = lax.rem(lax.axis_index("gz"), 2) == 0
    out, weight_grad, gamma_grad, beta_grad, high, low = outs
    main = jnp.where(even, part[...], other[...])
    slant = jnp.where(even, other[...], part[...])
    totals = main[:, taps : taps + 2]
    means = totals * (1.0 / count)
    scale = scales[0:chans, 2:3] * scales[chans : 2 * chans, 1:2]
    whole = scale * (main - means[:, 0:1] * slant)
    for tap in range(27):
        weight_grad[tap] = whole[:, tap * chans : (tap + 1) * chans]
    lane = lax.broadcasted_iota(jnp.int32, (chans, 128), 1)
    columns = jnp.where(
        lane == 0,
        scales[0:chans, 0:1],
        jnp.where(
            lane == 1,
            scales[chans : 2 * chans, 1:2],
            jnp.where(
                lane == 2,
                scales[0:chans, 2:3],
                jnp.where(
                    lane == 3,
                    scales[0:chans, 3:4],
                    jnp.where(lane == 4, totals[:, 0:1], totals[:, 1:2]),
                ),
            ),
        ),
    )
    table = jnp.concatenate([columns, jnp.zeros((128 - chans, 128), F32)], axis=0).T
    gamma_grad[...] = table[4:5, :chans]
    beta_grad[...] = table[5:6, :chans]
    factor = jnp.where(lax.broadcasted_iota(jnp.int32, (128, 128), 0) < 4, 1.0, 1.0 / count)
    table = table * factor
    across = [
        jnp.broadcast_to(along(table[at : at + 1], chans), (rows, 128)) for at in range(6)
    ]
    parts = [columns[:, at : at + 1] for at in range(4)] + [means[:, 0:1], means[:, 1:2]]
    down = [jnp.broadcast_to(one, (chans, size_z)) for one in parts]

    def mixed(pull, conv, mean, rstd, gain, shift, gamma_mean, beta_mean):
        grad, normed = slope(pull, conv, mean, rstd, gain, shift)
        return gain * rstd * (grad - beta_mean - normed * gamma_mean)

    edge_before = mixed(before[0:rows], before[rows : 2 * rows], *across)
    edge_after = mixed(after[0:rows], after[rows : 2 * rows], *across)
    for at in range(padded.shape[1] // group):
        edges = halo_block(edge_before, edge_after, at, size_z)
        for one in range(group):
            pair = at * group + one
            value = mixed(padded[0, pair], padded[1, pair], *down)
            put_shifts(pair, value, edges[one * chans : (one + 1) * chans], high, low)
    width = math.gcd(size_y, 8)
    both_now, top_now = both[...], top[...]
    stride = size_x * size_y

    def step(at, _):
        x, y = at // (size_y // width), (at % (size_y // width)) * width
        value = product(both_now, top_now, high, low, x, y, wide, width)
        for one in range(width):
            out[pl.ds(x * size_y + y + one, chans, stride=stride), :] = value[
                :, one * size_z : (one + 1) * size_z
            ]
        return 0

    lax.fori_loop(0, size_x * size_y // width, step, 0, unroll=True)


def total_over(keep, send):
    count_z = lax.axis_size("gz")
    assert count_z % 2 == 0
    pairs = [(i, i ^ 1) for i in range(count_z)]
    part = keep + lax.ppermute(send, "gz", pairs)
    for axis, step in (("gz", 2), ("gy", 1), ("gx", 1)):
        count = lax.axis_size(axis)
        assert count & (count - 1) == 0
        while step < count:
            part = part + lax.ppermute(part, axis, [(i, i ^ step) for i in range(count)])
            step *= 2
    return part, lax.ppermute(part, "gz", pairs)


def two_parts(table):
    top = lax.reduce_precision(table, 8, 7)
    rest = (table - top).astype(BF16)
    top = top.astype(BF16)
    return jnp.concatenate([top, rest], axis=0), top


def local_step(volume, weight, gamma, beta, cotangent):
    chans, size_x, size_y, size_z = volume.shape
    devices = 1
    for axis in AXES:
        devices *= lax.axis_size(axis)
    dims = (size_x, size_y, chans, size_z)
    count = float(size_x * size_y * size_z * devices)
    taps = 27 * chans
    tall = -(-taps // 128) * 128
    flat = (chans * size_x * size_y, size_z)
    store = call(functools.partial(split_faces, dims), face_shapes(1, dims))(volume.reshape(flat))
    padded, before, after = exchange(False, 1, dims, *store)
    both, top = two_parts(weight.transpose(0, 2, 3, 4, 1).reshape(chans, taps))
    back = weight[:, :, ::-1, ::-1, ::-1].transpose(1, 2, 3, 4, 0).reshape(chans, taps)
    back_both, back_top = two_parts(back)
    pairs = padded.shape[1]
    shifted = [pltpu.VMEM((pairs, 3 * chans, size_z), BF16)] * 2
    *store, stats = call(
        functools.partial(conv_kernel, dims),
        face_shapes(2, dims) + [((devices, 128), F32)],
        scratch=shifted,
    )(padded, before, after, both, top, cotangent.reshape(flat))
    stats = lax.all_to_all(stats, AXES, 0, 0, tiled=True)
    stats, back_both, back_top = lax.optimization_barrier((stats, back_both, back_top))
    keep, send, scales = call(
        functools.partial(act_kernel, dims, count),
        [((chans, tall), F32), ((chans, tall), F32), ((2 * chans, 128), F32)],
        scratch=shifted + [pltpu.VMEM((2, size_x, size_y, chans, size_z), F32)],
    )(store[0], padded, before, after, stats, gamma[None], beta[None])
    padded, before, after = exchange(True, 2, dims, *store)
    part, other = total_over(keep, send)
    input_grad, weight_grad, gamma_grad, beta_grad = call(
        functools.partial(grad_kernel, dims, count),
        [(flat, F32), ((27, chans, chans), F32), ((1, chans), F32), ((1, chans), F32)],
        scratch=shifted,
        last=True,
    )(padded, before, after, part, other, scales, back_both, back_top)
    weight_grad = weight_grad.reshape(3, 3, 3, chans, chans).transpose(3, 4, 0, 1, 2)
    return (
        input_grad.reshape(volume.shape),
        weight_grad,
        gamma_grad.reshape(chans),
        beta_grad.reshape(chans),
    )


def solution(mesh):
    return jax.shard_map(
        local_step,
        mesh=mesh,
        in_specs=(P(None, "gx", "gy", "gz"), P(), P(), P(), P(None, "gx", "gy", "gz")),
        out_specs=(P(None, "gx", "gy", "gz"), P(), P(), P()),
        check_vma=False,
    )
```
